512 devices in a mesh: grp: 16 (over y, x), ctx: 32 (over z, core).
Axes of the slice: x: 4, y: 4, z: 16, core: 2. Of those that a mesh axis runs over, the one named last changes fastest.
Arguments:
- queries: bfloat16 [262144, 1024], P(('grp', 'ctx')), may hold values from -6 to 6
- keys: bfloat16 [262144, 1024], P(('grp', 'ctx')), may hold values from -6 to 6
- values: bfloat16 [262144, 1024], P(('grp', 'ctx')), may hold values from -6 to 6
- level_weights: float32 [13, 8, 262144], P(None, None, ('grp', 'ctx')), may hold values from 0.1 to 1.5
Outputs:
- attended: bfloat16 [262144, 1024], P(('grp', 'ctx'))
The draws below stay inside these ranges and needn't reach their ends.
All inputs are finite; a program needn't handle non-finite values.
Results may differ from the reference program's by a relative error of at most 0.0095.
Values may be sent and summed in bfloat16 or wider, within the bound.
No kernel may reach another device: no remote copies, remote signals or barrier semaphores. Data moves between devices by JAX's collectives and lax.ppermute only.
A program may use at most 64 MiB of HBM per device.

```python
import math
import jax
import jax.numpy as jnp
from jax import lax

H = 8
DK = 128
STRETCH = 64
LEVELS = 13
TOK_DEV = 512
TOKENS = 262144
N_GRP = 16
N_CTX = 32


def block_scale(key, dims, cuts, low, top_value):
    gain = 1.0
    for dim, parts in cuts:
        steps = jax.random.uniform(jax.random.fold_in(jax.random.fold_in(key, 6), dim), (parts,), jnp.float32, low / len(cuts), top_value / len(cuts))
        gain = gain * jnp.repeat(jnp.exp(steps), dims[dim] // parts).reshape((-1,) + (1,) * (len(dims) - 1 - dim))
    return gain


def normal_values(own_key, dims, width, reach, split=(), held_as=jnp.bfloat16):
    values = jax.random.normal(own_key, dims, jnp.float32) * width
    if len(split) > 0:
        values = block_scale(own_key, dims, split, -0.22, 0.18) * values
    return jnp.clip(values, min=-reach, max=reach).astype(held_as)


def setup_inputs(seed: int = 0) -> dict:
    seeds = jax.random.split(jax.random.key(seed), 5)
    return {
        "queries": normal_values(seeds[0], (TOKENS, H * DK), 1.0, 6.0, ((0, 512),)),
        "keys": normal_values(seeds[1], (TOKENS, H * DK), 1.0, 6.0, ((0, 512),)),
        "values": normal_values(seeds[2], (TOKENS, H * DK), 1.0, 6.0, ((0, 512),)),
        "level_weights": jnp.clip(jnp.exp(math.log(1.5) - 2.7080502 * jax.random.uniform(seeds[3], (LEVELS, H, TOKENS), jnp.float32) ** block_scale(seeds[3], (LEVELS, H, TOKENS), ((2, 512),), -0.2, 0.2)), 0.1, 1.5),
    }


def level_factor(level_num):
    token_count = STRETCH if level_num == 0 else STRETCH * 2 ** (level_num - 1)
    return 1.0 / math.sqrt(DK * token_count)

def local_part(query_matrix, key_matrix, value_matrix, level_rows):
    row_count = query_matrix.shape[0]
    local_bits = (row_count // STRETCH).bit_length() - 1
    position = jnp.arange(row_count, dtype=jnp.int32)
    block_ids = position // STRETCH
    stretch_xor = jnp.bitwise_xor(block_ids[:, None], block_ids[None, :])
    level_ids = jnp.zeros((row_count, row_count), jnp.int32)
    for bit_num in range(local_bits):
        level_ids = level_ids + (stretch_xor >= 2 ** bit_num).astype(jnp.int32)
    causal = position[:, None] >= position[None, :]
    weight = jnp.zeros((level_rows.shape[1], row_count, row_count), jnp.float32)
    for level_num in range(local_bits + 1):
        picked = jnp.logical_and(level_ids == level_num, causal)
        weight = weight + jnp.where(picked[None], (level_rows[level_num] * level_factor(level_num))[:, :, None], 0.0)
    scores = jnp.einsum('thk,shk->hts', query_matrix.astype(jnp.float32), key_matrix.astype(jnp.float32))
    weighted = (scores * weight).astype(jnp.bfloat16)
    return jnp.einsum('hts,shv->thv', weighted.astype(jnp.float32), value_matrix.astype(jnp.float32))

def reference(queries, keys, values, level_weights):
    device_count = N_GRP * N_CTX
    ctx_bits = N_CTX.bit_length() - 1
    all_bits = device_count.bit_length() - 1
    local_bits = (TOK_DEV // STRETCH).bit_length() - 1
    query_all = queries.reshape(device_count, TOK_DEV, H, DK)
    key_all = keys.reshape(device_count, TOK_DEV, H, DK)
    value_all = values.reshape(device_count, TOK_DEV, H, DK)
    level_all = level_weights.reshape(LEVELS, H, device_count, TOK_DEV).transpose(2, 0, 1, 3)

    def block_state(coupled_rows):
        return jnp.einsum('pdx,pdo->dxo', coupled_rows[0].astype(jnp.float32), coupled_rows[1].astype(jnp.float32)).astype(jnp.bfloat16)
    states = lax.map(block_state, (key_all, value_all))
    tier_sums = []
    present_block = states.astype(jnp.float32)
    for bit_num in range(all_bits):
        tier_sums.append(present_block)
        paired = present_block.reshape(present_block.shape[0] // 2, 2, H, DK, DK)
        present_block = paired[:, 0] + paired[:, 1]
        if bit_num + 1 == ctx_bits:
            present_block = lax.optimization_barrier(present_block.astype(jnp.bfloat16)).astype(jnp.float32)

    def one_block(inputs):
        block_index, query_matrix, key_matrix, value_matrix, level_rows = inputs
        result = local_part(query_matrix, key_matrix, value_matrix, level_rows)
        for bit_num in range(all_bits):
            owner = jnp.right_shift(block_index, bit_num)
            left_index = jnp.maximum(owner - 1, 0).astype(jnp.int32)
            neighbor_block = lax.dynamic_index_in_dim(tier_sums[bit_num], left_index, 0, keepdims=False)
            neighbor_block = jnp.where(owner % 2 == 1, neighbor_block, 0.0).astype(jnp.bfloat16)
            outer_product = jnp.einsum('ryl,ylf->ryf', query_matrix.astype(jnp.float32), neighbor_block.astype(jnp.float32))
            level_num = 1 + local_bits + bit_num
            level_scale = (level_rows[level_num] * level_factor(level_num)).T
            result = result + outer_product * level_scale[:, :, None]
        return result.astype(jnp.bfloat16)
    block_ids = jnp.arange(device_count, dtype=jnp.int32)
    result = lax.map(one_block, (block_ids, query_all, key_all, value_all, level_all))
    return result.reshape(device_count * TOK_DEV, H * DK)
```

```python
import functools
import math

import jax
import jax.numpy as jnp
from jax import lax
from jax.experimental import pallas as pl
from jax.experimental.pallas import tpu as pltpu
from jax.sharding import PartitionSpec as P

DK = 128
STRETCH = 64
F32 = jnp.float32
BF16 = jnp.bfloat16


def level_factor(level_num):
    token_count = STRETCH if level_num == 0 else STRETCH * 2 ** (level_num - 1)
    return 1.0 / math.sqrt(DK * token_count)


def swap(block, axis, stride):
    count = lax.axis_size(axis)
    return lax.ppermute(block, axis, [(i, i ^ stride) for i in range(count)])


def on_chip(x):
    return pltpu.with_memory_space_constraint(x, pltpu.VMEM)


def state_kernel(half_ref, k_ref, v_ref, o_ref):
    o_ref[0] = lax.dot_general(
        k_ref[...], v_ref[...], (((0,), (0,)), ((), ())), preferred_element_type=F32
    ).astype(BF16)


def half_state(half, keys, values):
    rows, width = keys.shape
    heads = width // DK // 2
    spec = pl.BlockSpec((rows, DK), lambda i, h: (0, h[0] * heads + i))
    return pl.pallas_call(
        state_kernel,
        out_shape=jax.ShapeDtypeStruct((heads, DK, DK), BF16),
        grid_spec=pltpu.PrefetchScalarGridSpec(
            num_scalar_prefetch=1,
            grid=(heads,),
            in_specs=[spec, spec],
            out_specs=pl.BlockSpec((1, DK, DK), lambda i, h: (i, 0, 0)),
        ),
        cost_estimate=pl.CostEstimate(
            flops=2 * rows * DK * DK * heads, transcendentals=0, bytes_accessed=4 * rows * DK * heads
        ),
        name="half_state",
    )(half, keys, values)


def local_kernel(q_ref, k_ref, v_ref, s_ref, o_ref):
    rows = q_ref.shape[0]
    tile = 2 * STRETCH
    scale = s_ref[0].T
    row = lax.broadcasted_iota(jnp.int32, (tile, tile), 0)
    col = lax.broadcasted_iota(jnp.int32, (tile, tile), 1)
    low = jnp.logical_and(row >= STRETCH, col < STRETCH)
    same = jnp.logical_and(col <= row, jnp.logical_not(low))
    for r in range(rows // tile):
        at = pl.ds(r * tile, tile)
        query = q_ref[at, :]
        pick = scale[r * tile : (r + 1) * tile]
        span = (r + 1) * tile
        score = lax.dot_general(
            query, k_ref[pl.ds(0, span), :], (((1,), (1,)), ((), ())), preferred_element_type=F32
        )
        parts = []
        for c in range(r):
            level = 1 + (r ^ c).bit_length()
            parts.append(score[:, c * tile : (c + 1) * tile] * pick[:, level : level + 1])
        weight = jnp.where(same, pick[:, 0:1], jnp.where(low, pick[:, 1:2], 0.0))
        parts.append(score[:, r * tile :] * weight)
        weighted = jnp.concatenate([p.astype(BF16) for p in parts], axis=1)
        o_ref[at, :] = jnp.dot(weighted, v_ref[pl.ds(0, span), :], preferred_element_type=F32)


def local_part(queries, keys, values, scales):
    rows, width = queries.shape
    heads = width // DK
    spec = pl.BlockSpec((rows, DK), lambda h: (0, h))
    return pl.pallas_call(
        local_kernel,
        out_shape=jax.ShapeDtypeStruct((rows, width), F32),
        grid=(heads,),
        in_specs=[spec, spec, spec, pl.BlockSpec((1,) + scales.shape[1:], lambda h: (h, 0, 0))],
        out_specs=spec,
        cost_estimate=pl.CostEstimate(
            flops=4 * rows * rows * width, transcendentals=0, bytes_accessed=10 * rows * width
        ),
        name="local_part",
    )(queries, keys, values, scales)


def gather_kernel(bits, place_ref, first_ref, other_ref, *refs):
    ctx_refs, (all_ref, o_ref) = refs[:-2], refs[-2:]
    own = place_ref[0]
    o_ref[0] = jnp.where(place_ref[1] == 1, first_ref[...], other_ref[...])
    for b, ctx_ref in enumerate(ctx_refs):
        o_ref[1 + b] = ctx_ref[...]
    for b in range(bits):
        low = jnp.maximum(lax.shift_right_logical(own, b) - 1, 0) * 2**b
        for h in range(o_ref.shape[1]):
            total = all_ref[low, h].astype(F32)
            for i in range(1, 2**b):
                total = total + all_ref[low + i, h].astype(F32)
            o_ref[1 + len(ctx_refs) + b, h] = total.astype(BF16)


def gather_levels(place, first, other, ctx_levels, group_states):
    runs, heads = group_states.shape[:2]
    bits = runs.bit_length() - 1
    levels = 1 + len(ctx_levels) + bits
    return pl.pallas_call(
        functools.partial(gather_kernel, bits),
        out_shape=jax.ShapeDtypeStruct((levels, heads, DK, DK), BF16),
        in_specs=[pl.BlockSpec(memory_space=pltpu.SMEM)]
        + [pl.BlockSpec(memory_space=pltpu.VMEM)] * (3 + len(ctx_levels)),
        out_specs=pl.BlockSpec(memory_space=pltpu.VMEM),
        compiler_params=pltpu.CompilerParams(vmem_limit_bytes=16 << 20),
        name="gather_levels",
    )(place, first, other, *ctx_levels, on_chip(group_states))


def final_kernel(first_level, place_ref, q_ref, a_ref, s_ref, mine_ref, their_ref, o_ref):
    levels, half = mine_ref.shape[:2]
    for i in range(2 * half):
        states, n = (mine_ref, i) if i < half else (their_ref, i - half)
        side = place_ref[1] if i < half else 1 - place_ref[1]
        head = side * half + n
        at = pl.ds(pl.multiple_of(head * DK, DK), DK)
        scale = s_ref[head].T
        query = q_ref[:, at]
        total = a_ref[:, at]
        for j in range(levels):
            part = jnp.dot(query, states[j, n], preferred_element_type=F32)
            total = total + part * scale[:, first_level + j : first_level + j + 1]
        o_ref[:, at] = total.astype(BF16)


def final_part(place, queries, local, scales, mine, theirs, first_level):
    rows, width = queries.shape
    return pl.pallas_call(
        functools.partial(final_kernel, first_level),
        out_shape=jax.ShapeDtypeStruct((rows, width), BF16),
        in_specs=[pl.BlockSpec(memory_space=pltpu.SMEM)] + [pl.BlockSpec(memory_space=pltpu.VMEM)] * 5,
        out_specs=pl.BlockSpec(memory_space=pltpu.VMEM),
        compiler_params=pltpu.CompilerParams(vmem_limit_bytes=32 << 20),
        name="final_part",
    )(place, queries, local, scales, on_chip(mine), on_chip(theirs))


def on_device(queries, keys, values, level_weights):
    rows = queries.shape[0]
    local_bits = (rows // STRETCH).bit_length() - 1
    ctx_bits = lax.axis_size("ctx").bit_length() - 1
    grp_bits = lax.axis_size("grp").bit_length() - 1
    runs = lax.axis_size("grp")
    ctx_index = lax.axis_index("ctx").astype(jnp.int32)
    grp_index = lax.axis_index("grp").astype(jnp.int32)
    core = ctx_index % 2
    place = jnp.stack([grp_index, core])

    block = grp_index * lax.axis_size("ctx") + ctx_index
    level_ids = jnp.arange(level_weights.shape[0], dtype=jnp.int32)
    bit_of = jnp.maximum(level_ids - 1 - local_bits, 0)
    live = jnp.logical_or(level_ids <= local_bits, jnp.right_shift(block, bit_of) % 2 == 1)
    factor = jnp.asarray([level_factor(n) for n in range(level_weights.shape[0])], F32)
    gain = jnp.where(live, factor, 0.0)
    scales = jnp.transpose(level_weights * gain[:, None, None], (1, 0, 2))
    scales = jnp.pad(scales, ((0, 0), (0, -scales.shape[1] % 8), (0, 0)))

    send = half_state((1 - core)[None], keys, values)
    first = swap(send, "ctx", 1)
    keep = half_state(core[None], keys, values)
    running = keep.astype(F32) + first.astype(F32)
    ctx_levels = []
    for b in range(1, ctx_bits):
        partner = swap(running.astype(BF16), "ctx", 1 << b)
        ctx_levels.append(partner)
        running = running + partner.astype(F32)
    total = running.astype(BF16)
    group_states = lax.all_to_all(
        jnp.broadcast_to(total[None], (runs,) + total.shape), "grp", 0, 0, tiled=True
    )
    local = local_part(queries, keys, values, scales)
    group_states, local = lax.optimization_barrier((group_states, local))
    mine = gather_levels(place, first, keep, ctx_levels, group_states)
    theirs = swap(mine, "ctx", 1)
    return final_part(place, queries, local, scales, mine, theirs, 1 + local_bits)


def solution(mesh):
    return jax.shard_map(
        on_device,
        mesh=mesh,
        in_specs=(
            P(("grp", "ctx"), None),
            P(("grp", "ctx"), None),
            P(("grp", "ctx"), None),
            P(None, None, ("grp", "ctx")),
        ),
        out_specs=P(("grp", "ctx"), None),
        check_vma=False,
    )
```

```python
import functools
import math

import jax
import jax.numpy as jnp
from jax import lax
from jax.experimental import pallas as pl
from jax.experimental.pallas import tpu as pltpu
from jax.sharding import PartitionSpec as P

DK = 128
STRETCH = 64
F32 = jnp.float32
BF16 = jnp.bfloat16


def level_factor(level_num):
    token_count = STRETCH if level_num == 0 else STRETCH * 2 ** (level_num - 1)
    return 1.0 / math.sqrt(DK * token_count)


def swap(block, axis, stride):
    count = lax.axis_size(axis)
    return lax.ppermute(block, axis, [(i, i ^ stride) for i in range(count)])


def on_chip(x):
    return pltpu.with_memory_space_constraint(x, pltpu.VMEM)


def vmem_call(kernel, out_shapes, scalars, operands, name, limit_mib=32, flops=0):
    many = isinstance(out_shapes, (list, tuple))
    vmem = pl.BlockSpec(memory_space=pltpu.VMEM)
    moved = sum(x.size * x.dtype.itemsize for x in operands)
    return pl.pallas_call(
        kernel,
        out_shape=out_shapes,
        in_specs=[pl.BlockSpec(memory_space=pltpu.SMEM)] + [vmem] * len(operands),
        out_specs=[vmem] * len(out_shapes) if many else vmem,
        compiler_params=pltpu.CompilerParams(vmem_limit_bytes=limit_mib << 20),
        cost_estimate=pl.CostEstimate(flops=flops, transcendentals=0, bytes_accessed=moved),
        name=name,
    )(scalars, *operands)


def lanes(head):
    start = head * DK
    return pl.ds(start if isinstance(start, int) else pl.multiple_of(start, DK), DK)


def state_kernel(place_ref, k_ref, v_ref, send_ref, keep_ref):
    half = send_ref.shape[0]
    for o_ref, side in ((send_ref, 1 - place_ref[1]), (keep_ref, place_ref[1])):
        for n in range(half):
            at = lanes(side * half + n)
            o_ref[n] = lax.dot_general(
                v_ref[:, at], k_ref[:, at], (((0,), (0,)), ((), ())), preferred_element_type=F32
            ).astype(BF16)


def local_kernel(place_ref, q_ref, k_ref, v_ref, s_ref, o_ref):
    rows = q_ref.shape[0]
    tile = 2 * STRETCH
    key = lax.broadcasted_iota(jnp.int32, (tile, tile), 0)
    tok = lax.broadcasted_iota(jnp.int32, (tile, tile), 1)
    low = jnp.logical_and(tok >= STRETCH, key < STRETCH)
    same = jnp.logical_and(key <= tok, jnp.logical_not(low))
    for head in range(o_ref.shape[0]):
        at = lanes(head)
        value_t = v_ref[:, at].T
        for r in range(rows // tile):
            here = pl.ds(r * tile, tile)
            span = (r + 1) * tile
            score = lax.dot_general(
                k_ref[pl.ds(0, span), at], q_ref[here, at], (((1,), (1,)), ((), ())),
                preferred_element_type=F32,
            )
            parts = []
            for c in range(r):
                level = 1 + (r ^ c).bit_length()
                parts.append(score[c * tile : (c + 1) * tile] * s_ref[head, pl.ds(level, 1), here])
            weight = jnp.where(
                same, s_ref[head, pl.ds(0, 1), here], jnp.where(low, s_ref[head, pl.ds(1, 1), here], 0.0)
            )
            parts.append(score[r * tile :] * weight)
            weighted = jnp.concatenate([p.astype(BF16) for p in parts], axis=0)
            o_ref[head, :, here] = jnp.dot(value_t[:, :span], weighted, preferred_element_type=F32)


def sums_kernel(bits, place_ref, *refs):
    had, (all_ref, o_ref) = refs[:-2], refs[-2:]
    own = place_ref[0]
    for b, ref in enumerate(had):
        o_ref[b] = ref[0]
    for b in range(bits):
        low = jnp.maximum(lax.shift_right_logical(own, b) - 1, 0) * 2**b
        total = all_ref[low].astype(F32)
        for i in range(1, 2**b):
            total = total + all_ref[low + i].astype(F32)
        o_ref[len(had) + b] = total.astype(BF16)


def final_kernel(early, first_level, place_ref, q_ref, a_ref, s_ref, mine_ref, their_ref, o_ref):
    half = a_ref.shape[0] // 2
    late = mine_ref.shape[0] // half - early
    for states, side in ((mine_ref, place_ref[1]), (their_ref, 1 - place_ref[1])):
        for slot in range(half):
            n = place_ref[2] ^ (slot // 2 | slot % 2 * 2)
            head = side * half + n
            at = lanes(head)
            query = q_ref[:, at]
            total = a_ref[head]
            found = [states[level * half + n] for level in range(early)]
            found.append(states[pl.ds(early * half + slot * late, late)].reshape(late * DK, DK))
            part = lax.dot_general(
                jnp.concatenate(found, axis=0), query, (((1,), (1,)), ((), ())), preferred_element_type=F32
            )
            for j in range(early + late):
                total = total + part[j * DK : (j + 1) * DK] * s_ref[head, pl.ds(first_level + j, 1), :]
            o_ref[:, at] = total.T.astype(BF16)


def on_device(queries, keys, values, level_weights):
    rows, width = queries.shape
    heads = width // DK
    half = heads // 2
    local_bits = (rows // STRETCH).bit_length() - 1
    ctx_bits = lax.axis_size("ctx").bit_length() - 1
    runs = lax.axis_size("grp")
    grp_bits = runs.bit_length() - 1
    ctx_index = lax.axis_index("ctx").astype(jnp.int32)
    grp_index = lax.axis_index("grp").astype(jnp.int32)
    core = ctx_index & 1
    quarter = lax.shift_right_logical(ctx_index, 1) & 3
    place = jnp.stack([grp_index, core, quarter])

    block = grp_index * lax.axis_size("ctx") + ctx_index
    level_ids = jnp.arange(level_weights.shape[0], dtype=jnp.int32)
    bit_of = jnp.maximum(level_ids - 1 - local_bits, 0)
    live = jnp.logical_or(level_ids <= local_bits, jnp.right_shift(block, bit_of) % 2 == 1)
    factor = jnp.asarray([level_factor(n) for n in range(level_weights.shape[0])], F32)
    gain = jnp.where(live, factor, 0.0)
    scales = jnp.transpose(level_weights * gain[:, None, None], (1, 0, 2))
    scales = jnp.pad(scales, ((0, 0), (0, -scales.shape[1] % 8), (0, 0)))

    state = jax.ShapeDtypeStruct((half, DK, DK), BF16)
    send, keep = vmem_call(
        state_kernel, [state, state], place, [keys, values], "block_states", 16, 2 * rows * DK * width
    )
    first = swap(send, "ctx", 1)
    running = keep.astype(F32) + first.astype(F32)
    early = [jnp.where(core == 1, first, keep)]
    for b in (1, 2):
        early.append(swap(running.astype(BF16), "ctx", 1 << b))
        running = running + early[-1].astype(F32)

    running = lax.dynamic_slice_in_dim(running, quarter, 1, 0)
    late = []
    for b in range(3, ctx_bits):
        late.append(swap(running.astype(BF16), "ctx", 1 << b))
        running = running + late[-1].astype(F32)
    group_states = lax.all_to_all(
        jnp.broadcast_to(running.astype(BF16), (runs, DK, DK)), "grp", 0, 0, tiled=True
    )
    local = vmem_call(
        local_kernel,
        jax.ShapeDtypeStruct((heads, DK, rows), F32),
        place,
        [queries, keys, values, scales],
        "local_part",
        32,
        4 * rows * rows * width,
    )
    group_states, local = lax.optimization_barrier((group_states, local))
    levels = len(late) + grp_bits
    one = vmem_call(
        functools.partial(sums_kernel, grp_bits),
        jax.ShapeDtypeStruct((levels, DK, DK), BF16),
        place,
        [*late, on_chip(group_states)],
        "run_sums",
        16,
    )
    two = jnp.concatenate([one, swap(one, "ctx", 4)], axis=0)
    four = [two, swap(two, "ctx", 2)]
    mine = jnp.concatenate(early + four, axis=0)
    theirs = swap(mine, "ctx", 1)
    return vmem_call(
        functools.partial(final_kernel, len(early), 1 + local_bits),
        jax.ShapeDtypeStruct((rows, width), BF16),
        place,
        [queries, local, scales, on_chip(mine), on_chip(theirs)],
        "final_part",
        32,
        2 * rows * DK * width * (3 + levels),
    )


def solution(mesh):
    return jax.shard_map(
        on_device,
        mesh=mesh,
        in_specs=(
            P(("grp", "ctx"), None),
            P(("grp", "ctx"), None),
            P(("grp", "ctx"), None),
            P(None, None, ("grp", "ctx")),
        ),
        out_specs=P(("grp", "ctx"), None),
        check_vma=False,
    )
```

```python
import functools
import math

import jax
import jax.numpy as jnp
from jax import lax
from jax.experimental import pallas as pl
from jax.experimental.pallas import tpu as pltpu
from jax.sharding import PartitionSpec as P


DK = 128
STRETCH = 64
F32 = jnp.float32
BF16 = jnp.bfloat16


def level_factor(level_num):
    token_count = STRETCH if level_num == 0 else STRETCH * 2 ** (level_num - 1)
    return 1.0 / math.sqrt(DK * token_count)


def swap(block, axis, stride):
    count = lax.axis_size(axis)
    return lax.ppermute(block, axis, [(i, i ^ stride) for i in range(count)])


VMEM = pl.BlockSpec(memory_space=pltpu.VMEM)
HBM = pl.BlockSpec(memory_space=pltpu.HBM)


def on_chip(x):
    return pltpu.with_memory_space_constraint(x, pltpu.VMEM)


def in_hbm(x):
    return pltpu.with_memory_space_constraint(x, pltpu.HBM)


def states(count, dtype=BF16):
    return jax.ShapeDtypeStruct((count, DK, DK), dtype)


def my_place():
    run, at = lax.axis_index("grp"), lax.axis_index("ctx")
    right = lax.shift_right_logical
    return run, at & 1, right(at, 1) & 3, right(at, 3), run * lax.axis_size("ctx") + at


def kernel_call(kernel, name, outs, operands, *, limit=16, flops=0, spaces=None, **more):
    moved = sum(x.size * x.dtype.itemsize for x in operands)
    out_specs = more.pop("out_specs", None) or jax.tree.map(lambda _: VMEM, outs)
    return pl.pallas_call(
        kernel,
        out_shape=outs,
        in_specs=spaces or [VMEM] * len(operands),
        out_specs=out_specs,
        compiler_params=pltpu.CompilerParams(vmem_limit_bytes=limit << 20),
        cost_estimate=pl.CostEstimate(flops=flops, transcendentals=0, bytes_accessed=moved),
        name=name,
        **more,
    )(*operands)


def lanes(head):
    start = head * DK
    return pl.ds(start if isinstance(start, int) else pl.multiple_of(start, DK), DK)


def state_kernel(flip, k_hbm, v_hbm, o_ref, k_ref, v_ref, sems):
    width = k_ref.shape[1]
    at = pl.ds(pl.multiple_of((my_place()[1] ^ flip) * width, width), width)
    copies = [
        pltpu.make_async_copy(src.at[:, at], dst, sems.at[i])
        for i, (src, dst) in enumerate(((k_hbm, k_ref), (v_hbm, v_ref)))
    ]
    for copy in copies:
        copy.start()
    for copy in copies:
        copy.wait()
    for n in range(o_ref.shape[0]):
        o_ref[n] = lax.dot_general(
            v_ref[:, lanes(n)], k_ref[:, lanes(n)], (((0,), (0,)), ((), ())), preferred_element_type=F32
        ).astype(BF16)


def half_states(flip, keys, values, name):
    rows, width = keys.shape
    buffer = pltpu.VMEM((rows, width // 2), BF16)
    return kernel_call(
        functools.partial(state_kernel, flip),
        name,
        states(width // DK // 2),
        [in_hbm(keys), in_hbm(values)],
        flops=rows * DK * width,
        spaces=[HBM, HBM],
        scratch_shapes=[buffer, buffer, pltpu.SemaphoreType.DMA((2,))],
    )


def local_kernel(q_ref, k_ref, v_ref, w_ref, o_ref):
    rows = q_ref.shape[0]
    tile = 2 * STRETCH
    key = lax.broadcasted_iota(jnp.int32, (tile, tile), 0)
    tok = lax.broadcasted_iota(jnp.int32, (tile, tile), 1)
    low = jnp.logical_and(tok >= STRETCH, key < STRETCH)
    same = jnp.logical_and(key <= tok, jnp.logical_not(low))
    for head in range(o_ref.shape[0]):
        at = lanes(head)
        value_t = v_ref[:, at].T
        for r in range(rows // tile):
            here = pl.ds(r * tile, tile)
            span = (r + 1) * tile

            def scale(level):
                return w_ref[level, pl.ds(head, 1), here] * level_factor(level)

            score = lax.dot_general(
                k_ref[pl.ds(0, span), at], q_ref[here, at], (((1,), (1,)), ((), ())),
                preferred_element_type=F32,
            )
            parts = []
            for c in range(r):
                parts.append(score[c * tile : (c + 1) * tile] * scale(1 + (r ^ c).bit_length()))
            weight = jnp.where(same, scale(0), jnp.where(low, scale(1), 0.0))
            parts.append(score[r * tile :] * weight)
            weighted = jnp.concatenate([p.astype(BF16) for p in parts], axis=0)
            o_ref[head, :, here] = jnp.dot(value_t[:, :span], weighted, preferred_element_type=F32)


def pick_kernel(*refs):
    parts, o_ref = refs[:-1], refs[-1]
    n = my_place()[2]
    total = parts[0][n].astype(F32)
    for ref in parts[1:]:
        total = total + ref[n].astype(F32)
    for g in range(o_ref.shape[0]):
        o_ref[g] = total.astype(BF16)


def sibling_sums(own, all_ref, o_ref, first):
    for b in range(all_ref.shape[0].bit_length() - 1):
        low = jnp.maximum(lax.shift_right_logical(own, b) - 1, 0) * 2**b
        total = all_ref[low].astype(F32)
        for i in range(1, 2**b):
            total = total + all_ref[low + i].astype(F32)
        o_ref[first + b] = total.astype(BF16)


def group_kernel(all_ref, late_ref, o_ref):
    sibling_sums(my_place()[3], all_ref, late_ref, 0)
    total = all_ref[0].astype(F32)
    for g in range(1, all_ref.shape[0]):
        total = total + all_ref[g].astype(F32)
    for r in range(o_ref.shape[0]):
        o_ref[r] = total.astype(BF16)


def run_kernel(late_ref, all_ref, o_ref):
    had = late_ref.shape[0]
    o_ref[pl.ds(0, had)] = late_ref[...]
    sibling_sums(my_place()[0], all_ref, o_ref, had)


def pack_kernel(keep_ref, first_ref, one_ref, two_ref, late_ref, o_ref):
    half = keep_ref.shape[0]
    o_ref[pl.ds(0, half)] = jnp.where(my_place()[1] == 1, first_ref[...], keep_ref[...])
    o_ref[pl.ds(half, half)] = one_ref[...]
    o_ref[pl.ds(2 * half, half)] = two_ref[...]
    o_ref[pl.ds(3 * half, late_ref.shape[0])] = late_ref[...]


def slot_head(slot):
    return my_place()[2] ^ (slot // 2 | slot % 2 * 2)


def add_levels(q_ref, w_ref, total, head, found, bits, local_bits):
    part = lax.dot_general(found, q_ref[:, lanes(head)], (((1,), (1,)), ((), ())), preferred_element_type=F32)
    for i, bit in enumerate(bits):
        level = 1 + local_bits + bit
        live = (lax.shift_right_logical(my_place()[4], bit) & 1) == 1
        gain = jnp.where(live, level_factor(level), 0.0)
        total = total + part[i * DK : (i + 1) * DK] * (w_ref[level, pl.ds(head, 1), :] * gain)
    return total


def first_kernel(early, local_bits, q_ref, a_ref, w_ref, mine_ref, their_ref, o_ref):
    half = a_ref.shape[0] // 2
    late = mine_ref.shape[0] - early * half
    for ref, side in ((mine_ref, my_place()[1]), (their_ref, 1 - my_place()[1])):
        for slot in range(half):
            n = slot_head(slot)
            found = [ref[level * half + n] for level in range(early)]
            bits = list(range(early))
            if slot == 0:
                found.append(ref[pl.ds(early * half, late)].reshape(late * DK, DK))
                bits += range(early, early + late)
            head = side * half + n
            o_ref[head] = add_levels(
                q_ref, w_ref, a_ref[head], head, jnp.concatenate(found, axis=0), bits, local_bits
            )


def close_kernel(todo, early, local_bits, q_ref, a_ref, w_ref, *refs):
    count = 1 + max([op for _, _, op, _ in todo if op is not None])
    found_refs, (out_hbm, o_ref, sems) = refs[:count], refs[-3:]
    half = a_ref.shape[0] // 2
    late = min(ref.shape[0] for ref in found_refs)
    if len(todo) == 2:
        late = found_refs[0].shape[0] // 2
    copies = []
    for i, (other, slot, op, start) in enumerate(todo):
        side = 1 - my_place()[1] if other else my_place()[1]
        head = side * half + slot_head(slot)
        total = a_ref[head]
        if op is not None:
            found = found_refs[op][pl.ds(start * late, late)].reshape(late * DK, DK)
            bits = range(early, early + late)
            total = add_levels(q_ref, w_ref, total, head, found, bits, local_bits)
        o_ref[i] = total.T.astype(BF16)
        copies.append(pltpu.make_async_copy(o_ref.at[i], out_hbm.at[:, lanes(head)], sems.at[i]))
        copies[-1].start()
    for copy in copies:
        copy.wait()


def close_heads(todo, early, local_bits, queries, total, weights, found, name, before=None):
    rows, width = queries.shape
    operands = [queries, total, weights, *found] + ([] if before is None else [before])
    spaces = [VMEM] * (3 + len(found)) + ([] if before is None else [HBM])
    more = {} if before is None else {"input_output_aliases": {len(operands) - 1: 0}}
    return kernel_call(
        functools.partial(close_kernel, todo, early, local_bits),
        name,
        jax.ShapeDtypeStruct((rows, width), BF16),
        operands,
        limit=24,
        flops=12 * rows * DK * DK * len(todo),
        spaces=spaces,
        out_specs=HBM,
        scratch_shapes=[pltpu.VMEM((len(todo), rows, DK), BF16), pltpu.SemaphoreType.DMA((len(todo),))],
        **more,
    )


def on_device(queries, keys, values, level_weights):
    rows, width = queries.shape
    heads = width // DK
    half = heads // 2
    local_bits = (rows // STRETCH).bit_length() - 1
    blocks = lax.axis_size("ctx")
    runs = lax.axis_size("grp")
    groups = blocks // 8
    send = half_states(1, keys, values, "send_states")
    first = swap(send, "ctx", 1)
    keep = half_states(0, keys, values, "keep_states")
    running = keep.astype(F32) + first.astype(F32)
    one_z = swap(running.astype(BF16), "ctx", 2)
    running = running + one_z.astype(F32)
    two_z = swap(running.astype(BF16), "ctx", 4)

    picked = kernel_call(pick_kernel, "pick_head", states(groups), [keep, first, one_z, two_z])
    members = [[low + 8 * g for g in range(groups)] for low in range(8)]
    group_sums = lax.all_to_all(picked, "ctx", 0, 0, axis_index_groups=members, tiled=True)
    late, spread = kernel_call(
        group_kernel, "group_sums", [states(groups.bit_length() - 1), states(runs)], [group_sums]
    )
    run_states = lax.all_to_all(spread, "grp", 0, 0, tiled=True)
    local = kernel_call(
        local_kernel,
        "local_part",
        jax.ShapeDtypeStruct((heads, DK, rows), F32),
        [queries, keys, values, level_weights],
        limit=32,
        flops=4 * rows * rows * width,
    )
    run_states, local = lax.optimization_barrier((run_states, local))
    levels = late.shape[0] + runs.bit_length() - 1
    slot0 = kernel_call(run_kernel, "run_sums", states(levels), [late, run_states])

    early = 3
    slot1 = swap(slot0, "ctx", 4)
    mine0 = kernel_call(
        pack_kernel, "pack_levels", states(early * half + levels), [keep, first, one_z, two_z, slot0]
    )
    their0 = swap(mine0, "ctx", 1)
    slot23 = swap(jnp.concatenate([slot0, slot1], axis=0), "ctx", 2)
    their1 = swap(slot1, "ctx", 1)
    total = kernel_call(
        functools.partial(first_kernel, early, local_bits),
        "first_levels",
        local,
        [queries, local, level_weights, mine0, their0],
        limit=24,
        flops=2 * rows * DK * DK * (heads * early + 2 * levels),
    )
    slot23, total, their1 = lax.optimization_barrier((slot23, total, their1))
    their23 = swap(slot23, "ctx", 1)
    close = functools.partial(close_heads, early=early, local_bits=local_bits)
    first_heads = (
        (False, 0, None, 0), (True, 0, None, 0), (False, 1, 0, 0), (True, 1, 1, 0), (False, 2, 2, 0), (False, 3, 2, 1)
    )
    out = close(
        first_heads, queries=queries, total=total, weights=level_weights, found=[slot1, their1, slot23],
        name="close_first",
    )
    their23, out = lax.optimization_barrier((their23, out))
    return close(
        ((True, 2, 0, 0), (True, 3, 0, 1)), queries=queries, total=total, weights=level_weights, found=[their23],
        name="close_last", before=out,
    )


def solution(mesh):
    return jax.shard_map(
        on_device,
        mesh=mesh,
        in_specs=(
            P(("grp", "ctx"), None),
            P(("grp", "ctx"), None),
            P(("grp", "ctx"), None),
            P(None, None, ("grp", "ctx")),
        ),
        out_specs=P(("grp", "ctx"), None),
        check_vma=False,
    )
```

```python
import functools
import math

import jax
import jax.numpy as jnp
from jax import lax
from jax.experimental import pallas as pl
from jax.experimental.pallas import tpu as pltpu
from jax.sharding import PartitionSpec as P


DK = 128
STRETCH = 64
F32 = jnp.float32
BF16 = jnp.bfloat16


def level_factor(level_num):
    token_count = STRETCH if level_num == 0 else STRETCH * 2 ** (level_num - 1)
    return 1.0 / math.sqrt(DK * token_count)


def swap(block, axis, stride):
    count = lax.axis_size(axis)
    return lax.ppermute(block, axis, [(i, i ^ stride) for i in range(count)])


VMEM = pl.BlockSpec(memory_space=pltpu.VMEM)
HBM = pl.BlockSpec(memory_space=pltpu.HBM)


def in_hbm(x):
    return pltpu.with_memory_space_constraint(x, pltpu.HBM)


def states(count, dtype=BF16):
    return jax.ShapeDtypeStruct((count, DK, DK), dtype)


def my_place():
    run, at = lax.axis_index("grp"), lax.axis_index("ctx")
    right = lax.shift_right_logical
    return run, at & 1, right(at, 1) & 3, right(at, 3), run * lax.axis_size("ctx") + at


def kernel_call(kernel, outs, operands, *, limit=16, flops=0, spaces=None, **more):
    moved = sum(x.size * x.dtype.itemsize for x in operands)
    out_specs = more.pop("out_specs", None) or jax.tree.map(lambda _: VMEM, outs)
    return pl.pallas_call(
        kernel,
        out_shape=outs,
        in_specs=spaces or [VMEM] * len(operands),
        out_specs=out_specs,
        compiler_params=pltpu.CompilerParams(vmem_limit_bytes=limit << 20),
        cost_estimate=pl.CostEstimate(flops=flops, transcendentals=0, bytes_accessed=moved),
        **more,
    )(*operands)


def lanes(head):
    start = head * DK
    return pl.ds(start if isinstance(start, int) else pl.multiple_of(start, DK), DK)


def state_kernel(flip, k_hbm, v_hbm, o_ref, k_ref, v_ref, sems):
    width = k_ref.shape[1]
    at = pl.ds(pl.multiple_of((my_place()[1] ^ flip) * width, width), width)
    copies = [
        pltpu.make_async_copy(src.at[:, at], dst, sems.at[i])
        for i, (src, dst) in enumerate(((k_hbm, k_ref), (v_hbm, v_ref)))
    ]
    for copy in copies:
        copy.start()
    for copy in copies:
        copy.wait()
    for n in range(o_ref.shape[0]):
        o_ref[n] = lax.dot_general(
            v_ref[:, lanes(n)], k_ref[:, lanes(n)], (((0,), (0,)), ((), ())), preferred_element_type=F32
        ).astype(BF16)


def half_states(flip, keys, values):
    rows, width = keys.shape
    buffer = pltpu.VMEM((rows, width // 2), BF16)
    return kernel_call(
        functools.partial(state_kernel, flip),
        states(width // DK // 2),
        [in_hbm(keys), in_hbm(values)],
        flops=rows * DK * width,
        spaces=[HBM, HBM],
        scratch_shapes=[buffer, buffer, pltpu.SemaphoreType.DMA((2,))],
    )


def local_kernel(q_hbm, k_hbm, v_hbm, w_ref, o_ref, q_ref, k_ref, v_ref, sems):
    rows, width = q_ref.shape
    heads = o_ref.shape[0]
    copies = []
    for part in range(2):
        at = pl.ds(part * width // 2, width // 2)
        pairs = ((q_hbm, q_ref), (k_hbm, k_ref), (v_hbm, v_ref))
        copies.append(
            [pltpu.make_async_copy(x.at[:, at], y.at[:, at], sems.at[part, i]) for i, (x, y) in enumerate(pairs)]
        )
    for copy in copies[0] + copies[1]:
        copy.start()
    tile = 2 * STRETCH
    key = lax.broadcasted_iota(jnp.int32, (tile, tile), 0)
    tok = lax.broadcasted_iota(jnp.int32, (tile, tile), 1)
    low = jnp.logical_and(tok >= STRETCH, key < STRETCH)
    same = jnp.logical_and(key <= tok, jnp.logical_not(low))
    for head in range(heads):
        if head % (heads // 2) == 0:
            for copy in copies[head // (heads // 2)]:
                copy.wait()
        at = lanes(head)
        value_t = v_ref[:, at].T
        for r in range(rows // tile):
            here = pl.ds(r * tile, tile)
            span = (r + 1) * tile

            def scale(level):
                return w_ref[level, pl.ds(head, 1), here] * level_factor(level)

            score = lax.dot_general(
                k_ref[pl.ds(0, span), at], q_ref[here, at], (((1,), (1,)), ((), ())),
                preferred_element_type=F32,
            )
            parts = []
            for c in range(r):
                parts.append(score[c * tile : (c + 1) * tile] * scale(1 + (r ^ c).bit_length()))
            weight = jnp.where(same, scale(0), jnp.where(low, scale(1), 0.0))
            parts.append(score[r * tile :] * weight)
            weighted = jnp.concatenate([p.astype(BF16) for p in parts], axis=0)
            o_ref[head, :, here] = jnp.dot(value_t[:, :span], weighted, preferred_element_type=F32)


def local_part(queries, keys, values, weights):
    rows, width = queries.shape
    buffer = pltpu.VMEM((rows, width), BF16)
    return kernel_call(
        local_kernel,
        jax.ShapeDtypeStruct((width // DK, DK, rows), F32),
        [in_hbm(queries), in_hbm(keys), in_hbm(values), weights],
        limit=32,
        flops=4 * rows * rows * width,
        spaces=[HBM, HBM, HBM, VMEM],
        scratch_shapes=[buffer, buffer, buffer, pltpu.SemaphoreType.DMA((2, 3))],
    )


def split_kernel(keep_ref, first_ref, one_ref, o_ref, rest_ref):
    partner = my_place()[2] ^ 2

    def total(n):
        return (keep_ref[n].astype(F32) + first_ref[n].astype(F32) + one_ref[n].astype(F32)).astype(BF16)

    o_ref[0] = total(partner)
    for d in range(1, 1 + rest_ref.shape[0]):
        rest_ref[d - 1] = total(partner ^ d)


def pick_kernel(keep_ref, first_ref, one_ref, two_ref, o_ref):
    n = my_place()[2]
    total = keep_ref[n].astype(F32) + first_ref[n].astype(F32) + one_ref[n].astype(F32) + two_ref[0].astype(F32)
    for g in range(o_ref.shape[0]):
        o_ref[g] = total.astype(BF16)


def sibling_sums(own, all_ref, o_ref, first):
    for b in range(all_ref.shape[0].bit_length() - 1):
        low = jnp.maximum(lax.shift_right_logical(own, b) - 1, 0) * 2**b
        total = all_ref[low].astype(F32)
        for i in range(1, 2**b):
            total = total + all_ref[low + i].astype(F32)
        o_ref[first + b] = total.astype(BF16)


def group_kernel(all_ref, late_ref, o_ref):
    sibling_sums(my_place()[3], all_ref, late_ref, 0)
    total = all_ref[0].astype(F32)
    for g in range(1, all_ref.shape[0]):
        total = total + all_ref[g].astype(F32)
    for r in range(o_ref.shape[0]):
        o_ref[r] = total.astype(BF16)


def run_kernel(all_ref, o_ref):
    sibling_sums(my_place()[0], all_ref, o_ref, 0)


def pack_kernel(keep_ref, first_ref, one_ref, two_ref, rest_ref, *refs):
    o_ref = refs[-1]
    half = keep_ref.shape[0]
    n = my_place()[2]
    o_ref[pl.ds(0, half)] = jnp.where(my_place()[1] == 1, first_ref[...], keep_ref[...])
    o_ref[pl.ds(half, half)] = one_ref[...]
    o_ref[2 * half + n] = two_ref[0]
    for d in range(1, half):
        o_ref[2 * half + (n ^ d)] = rest_ref[d - 1]
    start = 3 * half
    for ref in refs[:-1]:
        o_ref[pl.ds(start, ref.shape[0])] = ref[...]
        start += ref.shape[0]


def slot_head(slot):
    return my_place()[2] ^ (slot // 2 | slot % 2 * 2)


def add_levels(q_ref, w_ref, total, head, found, bits, local_bits):
    part = lax.dot_general(found, q_ref[:, lanes(head)], (((1,), (1,)), ((), ())), preferred_element_type=F32)
    for i, bit in enumerate(bits):
        level = 1 + local_bits + bit
        live = (lax.shift_right_logical(my_place()[4], bit) & 1) == 1
        gain = jnp.where(live, level_factor(level), 0.0)
        total = total + part[i * DK : (i + 1) * DK] * (w_ref[level, pl.ds(head, 1), :] * gain)
    return total


def send_out(o_ref, sems, out_hbm, copies, total, head):
    i = len(copies)
    o_ref[i] = total.astype(BF16).T
    copies.append(pltpu.make_async_copy(o_ref.at[i], out_hbm.at[:, lanes(head)], sems.at[i]))
    copies[-1].start()


def near_kernel(mid, late, local_bits, q_ref, a_ref, w_ref, mine_ref, their_ref, t_ref, out_hbm, o_ref, sems):
    half = a_ref.shape[0] // 2
    copies = []
    for other, ref in enumerate((mine_ref, their_ref)):
        side = my_place()[1] ^ other
        for slot in range(half):
            n = slot_head(slot)
            head = side * half + n
            found = [ref[level * half + n] for level in range(3)]
            found.append(ref[pl.ds(3 * half + slot * mid, mid)].reshape(mid * DK, DK))
            bits = 3 + mid
            if slot < 2:
                found.append(ref[pl.ds((3 + mid) * half + slot * late, late)].reshape(late * DK, DK))
                bits += late
            found = jnp.concatenate(found, axis=0)
            total = add_levels(q_ref, w_ref, a_ref[head], head, found, range(bits), local_bits)
            if slot < 2:
                send_out(o_ref, sems, out_hbm, copies, total, head)
            else:
                t_ref[other * (half - 2) + slot - 2] = total
    for copy in copies:
        copy.wait()


def far_kernel(other, mid, late, local_bits, q_ref, t_ref, w_ref, found_ref, before_hbm, out_hbm, o_ref, sems):
    count = t_ref.shape[0] // 2
    copies = []
    for i in range(count):
        head = (my_place()[1] ^ other) * 2 * count + slot_head(2 + i)
        found = found_ref[pl.ds(i * late, late)].reshape(late * DK, DK)
        bits = range(3 + mid, 3 + mid + late)
        total = add_levels(q_ref, w_ref, t_ref[other * count + i], head, found, bits, local_bits)
        send_out(o_ref, sems, out_hbm, copies, total, head)
    for copy in copies:
        copy.wait()


def attend(queries, keys, values, level_weights):
    rows, width = queries.shape
    heads = width // DK
    half = heads // 2
    local_bits = (rows // STRETCH).bit_length() - 1
    blocks = lax.axis_size("ctx")
    runs = lax.axis_size("grp")
    groups = blocks // 8
    send = half_states(1, keys, values)
    first = swap(send, "ctx", 1)
    keep = half_states(0, keys, values)
    running = keep.astype(F32) + first.astype(F32)
    one_z = swap(running.astype(BF16), "ctx", 2)
    ahead, rest = kernel_call(split_kernel, [states(1), states(half - 1)], [keep, first, one_z])
    two_z = swap(ahead, "ctx", 4)
    two_rest = swap(rest, "ctx", 4)
    picked = kernel_call(pick_kernel, states(groups), [keep, first, one_z, two_z])
    members = [[low + 8 * g for g in range(groups)] for low in range(8)]
    group_sums = lax.all_to_all(picked, "ctx", 0, 0, axis_index_groups=members, tiled=True)
    mid = groups.bit_length() - 1
    mid0, spread = kernel_call(group_kernel, [states(mid), states(runs)], [group_sums])
    run_states = lax.all_to_all(spread, "grp", 0, 0, tiled=True)

    mid1 = swap(mid0, "ctx", 4)
    mid23 = swap(jnp.concatenate([mid0, mid1], axis=0), "ctx", 2)
    late = runs.bit_length() - 1
    slot0 = kernel_call(run_kernel, states(late), [run_states])

    slot1 = swap(slot0, "ctx", 4)
    local = local_part(queries, keys, values, level_weights)
    slot23 = swap(jnp.concatenate([slot0, slot1], axis=0), "ctx", 2)
    mine = kernel_call(
        pack_kernel,
        states((3 + mid) * half + 2 * late),
        [keep, first, one_z, two_z, two_rest, mid0, mid1, mid23, slot0, slot1],
    )
    theirs = swap(mine, "ctx", 1)
    out_type = jax.ShapeDtypeStruct((rows, width), BF16)
    out_buffers = lambda n: [pltpu.VMEM((n, rows, DK), BF16), pltpu.SemaphoreType.DMA((n,))]
    total, out = kernel_call(
        functools.partial(near_kernel, mid, late, local_bits),
        [jax.ShapeDtypeStruct((heads - 4, DK, rows), F32), out_type],
        [queries, local, level_weights, mine, theirs],
        limit=24,
        flops=2 * rows * DK * DK * (heads * (3 + mid) + 4 * late),
        out_specs=[VMEM, HBM],
        scratch_shapes=out_buffers(4),
    )

    def far(other, found, out):
        return kernel_call(
            functools.partial(far_kernel, other, mid, late, local_bits),
            out_type,
            [queries, total, level_weights, found, out],
            flops=4 * rows * DK * DK * late,
            spaces=[VMEM] * 4 + [HBM],
            out_specs=HBM,
            scratch_shapes=out_buffers(2),
            input_output_aliases={4: 0},
        )

    their23 = swap(slot23, "ctx", 1)
    return far(1, their23, far(0, slot23, out))


def solution(mesh):
    return jax.shard_map(
        attend,
        mesh=mesh,
        in_specs=(
            P(("grp", "ctx"), None),
            P(("grp", "ctx"), None),
            P(("grp", "ctx"), None),
            P(None, None, ("grp", "ctx")),
        ),
        out_specs=P(("grp", "ctx"), None),
        check_vma=False,
    )
```

```python
import functools
import math

import jax
import jax.numpy as jnp
from jax import lax
from jax.experimental import pallas as pl
from jax.experimental.pallas import tpu as pltpu
from jax.sharding import PartitionSpec as P


DK = 128
STRETCH = 64
F32 = jnp.float32
BF16 = jnp.bfloat16


def level_factor(level_num):
    token_count = STRETCH if level_num == 0 else STRETCH * 2 ** (level_num - 1)
    return 1.0 / math.sqrt(DK * token_count)


def swap(block, axis, stride):
    count = lax.axis_size(axis)
    return lax.ppermute(block, axis, [(i, i ^ stride) for i in range(count)])


VMEM = pl.BlockSpec(memory_space=pltpu.VMEM)
HBM = pl.BlockSpec(memory_space=pltpu.HBM)


def in_hbm(x):
    return pltpu.with_memory_space_constraint(x, pltpu.HBM)


def states(count, dtype=BF16):
    return jax.ShapeDtypeStruct((count, DK, DK), dtype)


def my_place():
    run, at = lax.axis_index("grp"), lax.axis_index("ctx")
    right = lax.shift_right_logical
    return run, at & 1, right(at, 1) & 3, right(at, 3), run * lax.axis_size("ctx") + at


def kernel_call(kernel, outs, operands, *, limit=16, flops=0, spaces=None, **more):
    moved = sum(x.size * x.dtype.itemsize for x in operands)
    out_specs = more.pop("out_specs", None) or jax.tree.map(lambda _: VMEM, outs)
    return pl.pallas_call(
        kernel,
        out_shape=outs,
        in_specs=spaces or [VMEM] * len(operands),
        out_specs=out_specs,
        compiler_params=pltpu.CompilerParams(vmem_limit_bytes=limit << 20),
        cost_estimate=pl.CostEstimate(flops=flops, transcendentals=0, bytes_accessed=moved),
        **more,
    )(*operands)


def lanes(head):
    start = head * DK
    return pl.ds(start if isinstance(start, int) else pl.multiple_of(start, DK), DK)


def state_kernel(flip, k_hbm, v_hbm, o_ref, k_ref, v_ref, sems):
    width = k_ref.shape[1]
    at = pl.ds(pl.multiple_of((my_place()[1] ^ flip) * width, width), width)
    copies = [
        pltpu.make_async_copy(src.at[:, at], dst, sems.at[i])
        for i, (src, dst) in enumerate(((k_hbm, k_ref), (v_hbm, v_ref)))
    ]
    for copy in copies:
        copy.start()
    for copy in copies:
        copy.wait()
    for n in range(o_ref.shape[0]):
        o_ref[n] = lax.dot_general(
            v_ref[:, lanes(n)], k_ref[:, lanes(n)], (((0,), (0,)), ((), ())), preferred_element_type=F32
        ).astype(BF16)


def half_states(flip, keys, values):
    rows, width = keys.shape
    buffer = pltpu.VMEM((rows, width // 2), BF16)
    return kernel_call(
        functools.partial(state_kernel, flip),
        states(width // DK // 2),
        [in_hbm(keys), in_hbm(values)],
        flops=rows * DK * width,
        spaces=[HBM, HBM],
        scratch_shapes=[buffer, buffer, pltpu.SemaphoreType.DMA((2,))],
    )


def local_kernel(q_hbm, k_hbm, v_hbm, w_ref, o_hbm, q_ref, k_ref, v_ref, o_ref, sems, out_sems):
    rows, width = q_ref.shape
    heads = o_ref.shape[0]
    copies = []
    for part in range(2):
        at = pl.ds(part * width // 2, width // 2)
        pairs = ((q_hbm, q_ref), (k_hbm, k_ref), (v_hbm, v_ref))
        copies.append(
            [pltpu.make_async_copy(x.at[:, at], y.at[:, at], sems.at[part, i]) for i, (x, y) in enumerate(pairs)]
        )
    for copy in copies[0] + copies[1]:
        copy.start()
    tile = 2 * STRETCH
    key = lax.broadcasted_iota(jnp.int32, (tile, tile), 0)
    tok = lax.broadcasted_iota(jnp.int32, (tile, tile), 1)
    low = jnp.logical_and(tok >= STRETCH, key < STRETCH)
    same = jnp.logical_and(key <= tok, jnp.logical_not(low))
    results = []
    for head in range(heads):
        if head % (heads // 2) == 0:
            for copy in copies[head // (heads // 2)]:
                copy.wait()
        at = lanes(head)
        value_t = v_ref[:, at].T
        for r in range(rows // tile):
            here = pl.ds(r * tile, tile)
            span = (r + 1) * tile

            def scale(level):
                return w_ref[level, pl.ds(head, 1), here] * level_factor(level)

            score = lax.dot_general(
                k_ref[pl.ds(0, span), at], q_ref[here, at], (((1,), (1,)), ((), ())),
                preferred_element_type=F32,
            )
            parts = []
            for c in range(r):
                parts.append(score[c * tile : (c + 1) * tile] * scale(1 + (r ^ c).bit_length()))
            weight = jnp.where(same, scale(0), jnp.where(low, scale(1), 0.0))
            parts.append(score[r * tile :] * weight)
            weighted = jnp.concatenate([p.astype(BF16) for p in parts], axis=0)
            o_ref[head, :, here] = jnp.dot(value_t[:, :span], weighted, preferred_element_type=F32)
        results.append(pltpu.make_async_copy(o_ref.at[head], o_hbm.at[head], out_sems.at[head]))
        results[-1].start()
    for copy in results:
        copy.wait()


def local_part(queries, keys, values, weights):
    rows, width = queries.shape
    buffer = pltpu.VMEM((rows, width), BF16)
    heads = width // DK
    return kernel_call(
        local_kernel,
        pltpu.HBM((heads, DK, rows), F32),
        [in_hbm(queries), in_hbm(keys), in_hbm(values), weights],
        limit=32,
        flops=4 * rows * rows * width,
        spaces=[HBM, HBM, HBM, VMEM],
        out_specs=HBM,
        scratch_shapes=[
            buffer,
            buffer,
            buffer,
            pltpu.VMEM((heads, DK, rows), F32),
            pltpu.SemaphoreType.DMA((2, 3)),
            pltpu.SemaphoreType.DMA((heads,)),
        ],
    )


def pair_kernel(keep_ref, first_ref, o_ref, rest_ref):
    partner = my_place()[2] ^ 1
    for i, d in enumerate((0, 2, 1, 3)):
        total = keep_ref[partner ^ d].astype(F32) + first_ref[partner ^ d].astype(F32)
        (o_ref if i < 2 else rest_ref)[i % 2] = total.astype(BF16)


def ahead_kernel(keep_ref, first_ref, one_ref, o_ref):
    n = my_place()[2] ^ 2
    o_ref[0] = (keep_ref[n].astype(F32) + first_ref[n].astype(F32) + one_ref[1].astype(F32)).astype(BF16)


def rest_kernel(keep_ref, first_ref, one_ref, other_ref, o_ref):
    n = my_place()[2]
    for i, (d, got) in enumerate(((3, other_ref[1]), (0, one_ref[0]), (1, other_ref[0]))):
        o_ref[i] = (keep_ref[n ^ d].astype(F32) + first_ref[n ^ d].astype(F32) + got.astype(F32)).astype(BF16)


def pick_kernel(keep_ref, first_ref, one_ref, two_ref, o_ref):
    n = my_place()[2]
    total = keep_ref[n].astype(F32) + first_ref[n].astype(F32) + one_ref[0].astype(F32) + two_ref[0].astype(F32)
    for g in range(o_ref.shape[0]):
        o_ref[g] = total.astype(BF16)


def sibling_sums(own, all_ref, o_ref, first):
    for b in range(all_ref.shape[0].bit_length() - 1):
        low = jnp.maximum(lax.shift_right_logical(own, b) - 1, 0) * 2**b
        total = all_ref[low].astype(F32)
        for i in range(1, 2**b):
            total = total + all_ref[low + i].astype(F32)
        o_ref[first + b] = total.astype(BF16)


def group_kernel(all_ref, late_ref, o_ref):
    sibling_sums(my_place()[3], all_ref, late_ref, 0)
    total = all_ref[0].astype(F32)
    for g in range(1, all_ref.shape[0]):
        total = total + all_ref[g].astype(F32)
    for r in range(o_ref.shape[0]):
        o_ref[r] = total.astype(BF16)


def run_kernel(all_ref, o_ref):
    sibling_sums(my_place()[0], all_ref, o_ref, 0)


def pack_kernel(keep_ref, first_ref, one_ref, other_ref, two_ref, rest_ref, *refs):
    o_ref = refs[-1]
    half = keep_ref.shape[0]
    n = my_place()[2]
    o_ref[pl.ds(0, half)] = jnp.where(my_place()[1] == 1, first_ref[...], keep_ref[...])
    for i in range(2):
        o_ref[half + (n ^ 2 * i)] = one_ref[i]
        o_ref[half + (n ^ 1 ^ 2 * i)] = other_ref[i]
    o_ref[2 * half + n] = two_ref[0]
    for d in range(1, half):
        o_ref[2 * half + (n ^ d)] = rest_ref[d - 1]
    start = 3 * half
    for ref in refs[:-1]:
        o_ref[pl.ds(start, ref.shape[0])] = ref[...]
        start += ref.shape[0]


def slot_head(slot):
    return my_place()[2] ^ (slot // 2 | slot % 2 * 2)


def add_levels(q_ref, w_ref, total, head, found, bits, local_bits):
    part = lax.dot_general(found, q_ref[:, lanes(head)], (((1,), (1,)), ((), ())), preferred_element_type=F32)
    for i, bit in enumerate(bits):
        level = 1 + local_bits + bit
        live = (lax.shift_right_logical(my_place()[4], bit) & 1) == 1
        gain = jnp.where(live, level_factor(level), 0.0)
        total = total + part[i * DK : (i + 1) * DK] * (w_ref[level, pl.ds(head, 1), :] * gain)
    return total


def send_out(o_ref, sems, out_hbm, copies, total, head):
    i = len(copies)
    o_ref[i] = total.astype(BF16).T
    copies.append(pltpu.make_async_copy(o_ref.at[i], out_hbm.at[:, lanes(head)], sems.at[i]))
    copies[-1].start()


def near_kernel(other, mid, late, local_bits, q_ref, a_hbm, w_ref, found_ref, *refs):
    t_ref, out_hbm, o_ref, sems, a_ref, a_sems = refs[-6:]
    half = a_ref.shape[0]
    locals_ = []
    for slot in range(half):
        head = (my_place()[1] ^ other) * half + slot_head(slot)
        locals_.append(pltpu.make_async_copy(a_hbm.at[head], a_ref.at[slot], a_sems.at[slot]))
        locals_[-1].start()
    copies = []
    for slot in range(half):
        n = slot_head(slot)
        head = (my_place()[1] ^ other) * half + n
        locals_[slot].wait()
        found = [found_ref[level * half + n] for level in range(3)]
        found.append(found_ref[pl.ds(3 * half + slot * mid, mid)].reshape(mid * DK, DK))
        bits = 3 + mid
        if slot < 2:
            found.append(found_ref[pl.ds((3 + mid) * half + slot * late, late)].reshape(late * DK, DK))
            bits += late
        found = jnp.concatenate(found, axis=0)
        total = add_levels(q_ref, w_ref, a_ref[slot], head, found, range(bits), local_bits)
        if slot < 2:
            send_out(o_ref, sems, out_hbm, copies, total, head)
        else:
            t_ref[slot - 2] = total
    for copy in copies:
        copy.wait()


def far_kernel(other, mid, late, local_bits, q_ref, t_ref, w_ref, found_ref, before_hbm, out_hbm, o_ref, sems):
    count = t_ref.shape[0]
    copies = []
    for i in range(count):
        head = (my_place()[1] ^ other) * 2 * count + slot_head(2 + i)
        found = found_ref[pl.ds(i * late, late)].reshape(late * DK, DK)
        bits = range(3 + mid, 3 + mid + late)
        total = add_levels(q_ref, w_ref, t_ref[i], head, found, bits, local_bits)
        send_out(o_ref, sems, out_hbm, copies, total, head)
    for copy in copies:
        copy.wait()


def attend(queries, keys, values, level_weights):
    rows, width = queries.shape
    heads = width // DK
    half = heads // 2
    local_bits = (rows // STRETCH).bit_length() - 1
    blocks = lax.axis_size("ctx")
    runs = lax.axis_size("grp")
    groups = blocks // 8
    send = half_states(1, keys, values)
    first = swap(send, "ctx", 1)
    keep = half_states(0, keys, values)
    pair, pair_rest = kernel_call(pair_kernel, [states(2), states(half - 2)], [keep, first])
    one_z = swap(pair, "ctx", 2)
    one_rest = swap(pair_rest, "ctx", 2)
    ahead = kernel_call(ahead_kernel, states(1), [keep, first, one_z])
    two_z = swap(ahead, "ctx", 4)
    rest = kernel_call(rest_kernel, states(half - 1), [keep, first, one_z, one_rest])
    two_rest = swap(rest, "ctx", 4)
    local = local_part(queries, keys, values, level_weights)
    picked = kernel_call(pick_kernel, states(groups), [keep, first, one_z, two_z])
    members = [[low + 8 * g for g in range(groups)] for low in range(8)]
    group_sums = lax.all_to_all(picked, "ctx", 0, 0, axis_index_groups=members, tiled=True)
    mid = groups.bit_length() - 1
    mid0, spread = kernel_call(group_kernel, [states(mid), states(runs)], [group_sums])
    run_states = lax.all_to_all(spread, "grp", 0, 0, tiled=True)

    mid1 = swap(mid0, "ctx", 4)
    mid23 = swap(jnp.concatenate([mid0, mid1], axis=0), "ctx", 2)
    late = runs.bit_length() - 1
    slot0 = kernel_call(run_kernel, states(late), [run_states])

    slot1 = swap(slot0, "ctx", 4)
    slot23 = swap(jnp.concatenate([slot0, slot1], axis=0), "ctx", 2)
    mine = kernel_call(
        pack_kernel,
        states((3 + mid) * half + 2 * late),
        [keep, first, one_z, one_rest, two_z, two_rest, mid0, mid1, mid23, slot0, slot1],
    )
    theirs = swap(mine, "ctx", 1)
    out_type = jax.ShapeDtypeStruct((rows, width), BF16)
    out_buffers = lambda n: [pltpu.VMEM((n, rows, DK), BF16), pltpu.SemaphoreType.DMA((n,))]

    def near(other, found, before):
        return kernel_call(
            functools.partial(near_kernel, other, mid, late, local_bits),
            [jax.ShapeDtypeStruct((half - 2, DK, rows), F32), out_type],
            [queries, in_hbm(local), level_weights, found, *before],
            limit=24,
            flops=2 * rows * DK * DK * (half * (3 + mid) + 2 * late),
            spaces=[VMEM, HBM, VMEM, VMEM] + [HBM] * len(before),
            out_specs=[VMEM, HBM],
            scratch_shapes=out_buffers(2) + [pltpu.VMEM((half, DK, rows), F32), pltpu.SemaphoreType.DMA((half,))],
            input_output_aliases={4: 1} if before else {},
        )

    def far(other, total, found, before):
        return kernel_call(
            functools.partial(far_kernel, other, mid, late, local_bits),
            out_type,
            [queries, total, level_weights, found, before],
            flops=4 * rows * DK * DK * late,
            spaces=[VMEM] * 4 + [HBM],
            out_specs=HBM,
            scratch_shapes=out_buffers(2),
            input_output_aliases={4: 0},
        )

    own_total, out = near(0, mine, [])
    other_total, out = near(1, theirs, [out])
    their23 = swap(slot23, "ctx", 1)
    out = far(0, own_total, slot23, out)
    return far(1, other_total, their23, out)


def solution(mesh):
    return jax.shard_map(
        attend,
        mesh=mesh,
        in_specs=(
            P(("grp", "ctx"), None),
            P(("grp", "ctx"), None),
            P(("grp", "ctx"), None),
            P(None, None, ("grp", "ctx")),
        ),
        out_specs=P(("grp", "ctx"), None),
        check_vma=False,
    )
```

```python
import functools
import math

import jax
import jax.numpy as jnp
from jax import lax
from jax.experimental import pallas as pl
from jax.experimental.pallas import tpu as pltpu
from jax.sharding import PartitionSpec as P


DK = 128
STRETCH = 64
F32 = jnp.float32
BF16 = jnp.bfloat16


def level_factor(level_num):
    token_count = STRETCH if level_num == 0 else STRETCH * 2 ** (level_num - 1)
    return 1.0 / math.sqrt(DK * token_count)


def swap(block, axis, stride):
    count = lax.axis_size(axis)
    return lax.ppermute(block, axis, [(i, i ^ stride) for i in range(count)])


VMEM = pl.BlockSpec(memory_space=pltpu.VMEM)
HBM = pl.BlockSpec(memory_space=pltpu.HBM)


def in_hbm(x):
    return pltpu.with_memory_space_constraint(x, pltpu.HBM)


def states(count, dtype=BF16):
    return jax.ShapeDtypeStruct((count, DK, DK), dtype)


def my_place():
    run, at = lax.axis_index("grp"), lax.axis_index("ctx")
    right = lax.shift_right_logical
    return run, at & 1, right(at, 1) & 3, right(at, 3), run * lax.axis_size("ctx") + at


def kernel_call(kernel, outs, operands, *, limit=16, flops=0, spaces=None, **more):
    moved = sum(x.size * x.dtype.itemsize for x in operands)
    out_specs = more.pop("out_specs", None) or jax.tree.map(lambda _: VMEM, outs)
    return pl.pallas_call(
        kernel,
        out_shape=outs,
        in_specs=spaces or [VMEM] * len(operands),
        out_specs=out_specs,
        compiler_params=pltpu.CompilerParams(vmem_limit_bytes=limit << 20),
        cost_estimate=pl.CostEstimate(flops=flops, transcendentals=0, bytes_accessed=moved),
        **more,
    )(*operands)


def lanes(head):
    start = head * DK
    return pl.ds(start if isinstance(start, int) else pl.multiple_of(start, DK), DK)


def fetch(pairs, side, sems):
    copies = []
    for i, (src, dst) in enumerate(pairs):
        width = dst.shape[1]
        at = pl.ds(pl.multiple_of(side * width, width), width)
        copies.append(pltpu.make_async_copy(src.at[:, at], dst, sems.at[i]))
        copies[-1].start()
    return copies


def put_states(k_ref, v_ref, o_ref):
    for n in range(o_ref.shape[0]):
        o_ref[n] = lax.dot_general(
            v_ref[:, lanes(n)], k_ref[:, lanes(n)], (((0,), (0,)), ((), ())), preferred_element_type=F32
        ).astype(BF16)


def send_kernel(k_hbm, v_hbm, o_ref, own_k_ref, own_v_ref, k_ref, v_ref, sems, own_sems):
    copies = fetch(((k_hbm, k_ref), (v_hbm, v_ref)), 1 - my_place()[1], sems)
    own = fetch(((k_hbm, own_k_ref), (v_hbm, own_v_ref)), my_place()[1], own_sems)
    for copy in copies:
        copy.wait()
    put_states(k_ref, v_ref, o_ref)
    for copy in own:
        copy.wait()


def send_states(keys, values):
    rows, width = keys.shape
    half = jax.ShapeDtypeStruct((rows, width // 2), BF16)
    buffer = pltpu.VMEM(half.shape, BF16)
    two = pltpu.SemaphoreType.DMA((2,))
    return kernel_call(
        send_kernel,
        [states(width // DK // 2), half, half],
        [in_hbm(keys), in_hbm(values)],
        flops=rows * DK * width,
        spaces=[HBM, HBM],
        scratch_shapes=[buffer, buffer, two, two],
    )


def local_kernel(other, q_hbm, k_hbm, v_hbm, w_ref, o_ref, q_ref, k_ref, v_ref, sems):
    side = my_place()[1] ^ other
    copies = fetch(((q_hbm, q_ref), (k_hbm, k_ref), (v_hbm, v_ref)), side, sems)
    rows = q_ref.shape[0]
    half = o_ref.shape[0]
    tile = 2 * STRETCH
    key = lax.broadcasted_iota(jnp.int32, (tile, tile), 0)
    tok = lax.broadcasted_iota(jnp.int32, (tile, tile), 1)
    low = jnp.logical_and(tok >= STRETCH, key < STRETCH)
    same = jnp.logical_and(key <= tok, jnp.logical_not(low))
    for copy in copies:
        copy.wait()
    for n in range(half):
        at = lanes(n)
        head = side * half + n
        value_t = v_ref[:, at].T
        levels = 1 + (rows // STRETCH).bit_length() - 1
        scales = [w_ref[level, pl.ds(head, 1), :] * level_factor(level) for level in range(levels)]
        for r in range(rows // tile):
            here = pl.ds(r * tile, tile)
            span = (r + 1) * tile
            scale = lambda level: scales[level][:, r * tile : (r + 1) * tile]
            score = lax.dot_general(
                k_ref[pl.ds(0, span), at], q_ref[here, at], (((1,), (1,)), ((), ())),
                preferred_element_type=F32,
            )
            parts = []
            for c in range(r):
                parts.append(score[c * tile : (c + 1) * tile] * scale(1 + (r ^ c).bit_length()))
            weight = jnp.where(same, scale(0), jnp.where(low, scale(1), 0.0))
            parts.append(score[r * tile :] * weight)
            weighted = jnp.concatenate([p.astype(BF16) for p in parts], axis=0)
            o_ref[n, :, here] = jnp.dot(value_t[:, :span], weighted, preferred_element_type=F32)


def local_part(other, queries, keys, values, weights):
    rows, width = queries.shape
    buffer = pltpu.VMEM((rows, width // 2), BF16)
    return kernel_call(
        functools.partial(local_kernel, other),
        jax.ShapeDtypeStruct((width // DK // 2, DK, rows), F32),
        [in_hbm(queries), in_hbm(keys), in_hbm(values), weights],
        flops=2 * rows * rows * width,
        spaces=[HBM, HBM, HBM, VMEM],
        scratch_shapes=[buffer, buffer, buffer, pltpu.SemaphoreType.DMA((3,))],
    )


def pair_kernel(keep_ref, first_ref, o_ref, rest_ref):
    partner = my_place()[2] ^ 1
    for i, d in enumerate((0, 2, 1, 3)):
        total = keep_ref[partner ^ d].astype(F32) + first_ref[partner ^ d].astype(F32)
        (o_ref if i < 2 else rest_ref)[i % 2] = total.astype(BF16)


def ahead_kernel(keep_ref, first_ref, one_ref, o_ref):
    n = my_place()[2] ^ 2
    o_ref[0] = (keep_ref[n].astype(F32) + first_ref[n].astype(F32) + one_ref[1].astype(F32)).astype(BF16)


def rest_kernel(keep_ref, first_ref, one_ref, other_ref, o_ref):
    n = my_place()[2]
    for i, (d, got) in enumerate(((3, other_ref[1]), (0, one_ref[0]), (1, other_ref[0]))):
        o_ref[i] = (keep_ref[n ^ d].astype(F32) + first_ref[n ^ d].astype(F32) + got.astype(F32)).astype(BF16)


def pick_kernel(keep_ref, first_ref, one_ref, two_ref, o_ref):
    n = my_place()[2]
    total = keep_ref[n].astype(F32) + first_ref[n].astype(F32) + one_ref[0].astype(F32) + two_ref[0].astype(F32)
    for g in range(o_ref.shape[0]):
        o_ref[g] = total.astype(BF16)


def sibling_sums(own, all_ref, o_ref, first):
    for b in range(all_ref.shape[0].bit_length() - 1):
        low = jnp.maximum(lax.shift_right_logical(own, b) - 1, 0) * 2**b
        total = all_ref[low].astype(F32)
        for i in range(1, 2**b):
            total = total + all_ref[low + i].astype(F32)
        o_ref[first + b] = total.astype(BF16)


def group_kernel(all_ref, late_ref, o_ref):
    sibling_sums(my_place()[3], all_ref, late_ref, 0)
    total = all_ref[0].astype(F32)
    for g in range(1, all_ref.shape[0]):
        total = total + all_ref[g].astype(F32)
    for r in range(o_ref.shape[0]):
        o_ref[r] = total.astype(BF16)


def run_kernel(all_ref, o_ref):
    sibling_sums(my_place()[0], all_ref, o_ref, 0)


def pack_kernel(keep_ref, first_ref, one_ref, other_ref, two_ref, rest_ref, *refs):
    o_ref = refs[-1]
    half = keep_ref.shape[0]
    n = my_place()[2]
    o_ref[pl.ds(0, half)] = jnp.where(my_place()[1] == 1, first_ref[...], keep_ref[...])
    for i in range(2):
        o_ref[half + (n ^ 2 * i)] = one_ref[i]
        o_ref[half + (n ^ 1 ^ 2 * i)] = other_ref[i]
    o_ref[2 * half + n] = two_ref[0]
    for d in range(1, half):
        o_ref[2 * half + (n ^ d)] = rest_ref[d - 1]
    start = 3 * half
    for ref in refs[:-1]:
        o_ref[pl.ds(start, ref.shape[0])] = ref[...]
        start += ref.shape[0]


def slot_head(slot):
    return my_place()[2] ^ (slot // 2 | slot % 2 * 2)


def add_levels(q_ref, w_ref, total, head, found, bits, local_bits):
    part = lax.dot_general(found, q_ref[:, lanes(head)], (((1,), (1,)), ((), ())), preferred_element_type=F32)
    for i, bit in enumerate(bits):
        level = 1 + local_bits + bit
        live = (lax.shift_right_logical(my_place()[4], bit) & 1) == 1
        gain = jnp.where(live, level_factor(level), 0.0)
        total = total + part[i * DK : (i + 1) * DK] * (w_ref[level, pl.ds(head, 1), :] * gain)
    return total


def send_out(o_ref, sems, out_hbm, copies, total, head):
    i = len(copies)
    o_ref[i] = total.astype(BF16).T
    copies.append(pltpu.make_async_copy(o_ref.at[i], out_hbm.at[:, lanes(head)], sems.at[i]))
    copies[-1].start()


def near_kernel(other, mid, late, local_bits, q_ref, a_ref, w_ref, found_ref, *refs):
    t_ref, out_hbm, o_ref, sems = refs[-4:]
    half = a_ref.shape[0]
    copies = []
    for slot in range(half):
        n = slot_head(slot)
        head = (my_place()[1] ^ other) * half + n
        found = [found_ref[level * half + n] for level in range(3)]
        found.append(found_ref[pl.ds(3 * half + slot * mid, mid)].reshape(mid * DK, DK))
        bits = 3 + mid
        if slot < 2:
            found.append(found_ref[pl.ds((3 + mid) * half + slot * late, late)].reshape(late * DK, DK))
            bits += late
        found = jnp.concatenate(found, axis=0)
        total = add_levels(q_ref, w_ref, a_ref[n], head, found, range(bits), local_bits)
        if slot < 2:
            send_out(o_ref, sems, out_hbm, copies, total, head)
        else:
            t_ref[slot - 2] = total
    for copy in copies:
        copy.wait()


def far_kernel(other, mid, late, local_bits, q_ref, t_ref, w_ref, found_ref, before_hbm, out_hbm, o_ref, sems):
    count = t_ref.shape[0]
    copies = []
    for i in range(count):
        head = (my_place()[1] ^ other) * 2 * count + slot_head(2 + i)
        found = found_ref[pl.ds(i * late, late)].reshape(late * DK, DK)
        bits = range(3 + mid, 3 + mid + late)
        total = add_levels(q_ref, w_ref, t_ref[i], head, found, bits, local_bits)
        send_out(o_ref, sems, out_hbm, copies, total, head)
    for copy in copies:
        copy.wait()


def attend(queries, keys, values, level_weights):
    rows, width = queries.shape
    heads = width // DK
    half = heads // 2
    local_bits = (rows // STRETCH).bit_length() - 1
    blocks = lax.axis_size("ctx")
    runs = lax.axis_size("grp")
    groups = blocks // 8
    send, own_keys, own_values = send_states(keys, values)
    first = swap(send, "ctx", 1)
    keep = kernel_call(put_states, states(half), [own_keys, own_values], flops=rows * DK * width)
    pair, pair_rest = kernel_call(pair_kernel, [states(2), states(half - 2)], [keep, first])
    one_z = swap(pair, "ctx", 2)
    one_rest = swap(pair_rest, "ctx", 2)
    ahead = kernel_call(ahead_kernel, states(1), [keep, first, one_z])
    two_z = swap(ahead, "ctx", 4)
    rest = kernel_call(rest_kernel, states(half - 1), [keep, first, one_z, one_rest])
    two_rest = swap(rest, "ctx", 4)
    locals_ = [local_part(other, queries, keys, values, level_weights) for other in (0, 1)]
    picked = kernel_call(pick_kernel, states(groups), [keep, first, one_z, two_z])
    members = [[low + 8 * g for g in range(groups)] for low in range(8)]
    group_sums = lax.all_to_all(picked, "ctx", 0, 0, axis_index_groups=members, tiled=True)
    mid = groups.bit_length() - 1
    mid0, spread = kernel_call(group_kernel, [states(mid), states(runs)], [group_sums])
    run_states = lax.all_to_all(spread, "grp", 0, 0, tiled=True)

    mid1 = swap(mid0, "ctx", 4)
    mid23 = swap(jnp.concatenate([mid0, mid1], axis=0), "ctx", 2)
    late = runs.bit_length() - 1
    slot0 = kernel_call(run_kernel, states(late), [run_states])

    slot1 = swap(slot0, "ctx", 4)
    slot23 = swap(jnp.concatenate([slot0, slot1], axis=0), "ctx", 2)
    mine = kernel_call(
        pack_kernel,
        states((3 + mid) * half + 2 * late),
        [keep, first, one_z, one_rest, two_z, two_rest, mid0, mid1, mid23, slot0, slot1],
    )
    theirs = swap(mine, "ctx", 1)
    out_type = jax.ShapeDtypeStruct((rows, width), BF16)
    out_buffers = lambda n: [pltpu.VMEM((n, rows, DK), BF16), pltpu.SemaphoreType.DMA((n,))]

    def near(other, found, before):
        return kernel_call(
            functools.partial(near_kernel, other, mid, late, local_bits),
            [jax.ShapeDtypeStruct((half - 2, DK, rows), F32), out_type],
            [queries, locals_[other], level_weights, found, *before],
            limit=24,
            flops=2 * rows * DK * DK * (half * (3 + mid) + 2 * late),
            spaces=[VMEM] * 4 + [HBM] * len(before),
            out_specs=[VMEM, HBM],
            scratch_shapes=out_buffers(2),
            input_output_aliases={4: 1} if before else {},
        )

    def far(other, total, found, before):
        return kernel_call(
            functools.partial(far_kernel, other, mid, late, local_bits),
            out_type,
            [queries, total, level_weights, found, before],
            flops=4 * rows * DK * DK * late,
            spaces=[VMEM] * 4 + [HBM],
            out_specs=HBM,
            scratch_shapes=out_buffers(2),
            input_output_aliases={4: 0},
        )

    own_total, out = near(0, mine, [])
    other_total, out = near(1, theirs, [out])
    their23 = swap(slot23, "ctx", 1)
    out = far(0, own_total, slot23, out)
    return far(1, other_total, their23, out)


def solution(mesh):
    return jax.shard_map(
        attend,
        mesh=mesh,
        in_specs=(
            P(("grp", "ctx"), None),
            P(("grp", "ctx"), None),
            P(("grp", "ctx"), None),
            P(None, None, ("grp", "ctx")),
        ),
        out_specs=P(("grp", "ctx"), None),
        check_vma=False,
    )
```

```python
import functools
import math

import jax
import jax.numpy as jnp
from jax import lax
from jax.experimental import pallas as pl
from jax.experimental.pallas import tpu as pltpu
from jax.sharding import PartitionSpec as P


DK = 128
STRETCH = 64
F32 = jnp.float32
BF16 = jnp.bfloat16


def level_factor(level_num):
    token_count = STRETCH if level_num == 0 else STRETCH * 2 ** (level_num - 1)
    return 1.0 / math.sqrt(DK * token_count)


def swap(block, axis, stride):
    count = lax.axis_size(axis)
    return lax.ppermute(block, axis, [(i, i ^ stride) for i in range(count)])


VMEM = pl.BlockSpec(memory_space=pltpu.VMEM)
HBM = pl.BlockSpec(memory_space=pltpu.HBM)


def in_hbm(x):
    return pltpu.with_memory_space_constraint(x, pltpu.HBM)


def states(count, dtype=BF16):
    return jax.ShapeDtypeStruct((count, DK, DK), dtype)


def my_place():
    run, at = lax.axis_index("grp"), lax.axis_index("ctx")
    right = lax.shift_right_logical
    return run, at & 1, right(at, 1) & 3, right(at, 3), run * lax.axis_size("ctx") + at


def kernel_call(kernel, outs, operands, *, limit=16, flops=0, spaces=None, **more):
    moved = sum(x.size * x.dtype.itemsize for x in operands)
    out_specs = more.pop("out_specs", None) or jax.tree.map(lambda _: VMEM, outs)
    return pl.pallas_call(
        kernel,
        out_shape=outs,
        in_specs=spaces or [VMEM] * len(operands),
        out_specs=out_specs,
        compiler_params=pltpu.CompilerParams(vmem_limit_bytes=limit << 20),
        cost_estimate=pl.CostEstimate(flops=flops, transcendentals=0, bytes_accessed=moved),
        **more,
    )(*operands)


def lanes(head):
    start = head * DK
    return pl.ds(start if isinstance(start, int) else pl.multiple_of(start, DK), DK)


def fetch(pairs, side, sems, parts=1):
    copies = []
    for part in range(parts):
        for i, (src, dst) in enumerate(pairs):
            width = dst.shape[1] // parts
            at = pl.ds(pl.multiple_of((side * parts + part) * width, width), width)
            to = dst.at[:, pl.ds(part * width, width)]
            copies.append(pltpu.make_async_copy(src.at[:, at], to, sems.at[part * len(pairs) + i]))
            copies[-1].start()
    return copies


def put_states(k_ref, v_ref, o_ref):
    for n in range(o_ref.shape[0]):
        o_ref[n] = lax.dot_general(
            v_ref[:, lanes(n)], k_ref[:, lanes(n)], (((0,), (0,)), ((), ())), preferred_element_type=F32
        ).astype(BF16)


def send_kernel(k_hbm, v_hbm, o_ref, own_k_ref, own_v_ref, k_ref, v_ref, sems, own_sems):
    copies = fetch(((k_hbm, k_ref), (v_hbm, v_ref)), 1 - my_place()[1], sems)
    own = fetch(((k_hbm, own_k_ref), (v_hbm, own_v_ref)), my_place()[1], own_sems)
    for copy in copies:
        copy.wait()
    put_states(k_ref, v_ref, o_ref)
    for copy in own:
        copy.wait()


def send_states(keys, values):
    rows, width = keys.shape
    half = jax.ShapeDtypeStruct((rows, width // 2), BF16)
    buffer = pltpu.VMEM(half.shape, BF16)
    two = pltpu.SemaphoreType.DMA((2,))
    return kernel_call(
        send_kernel,
        [states(width // DK // 2), half, half],
        [in_hbm(keys), in_hbm(values)],
        flops=rows * DK * width,
        spaces=[HBM, HBM],
        scratch_shapes=[buffer, buffer, two, two],
    )


def local_kernel(other, q_hbm, k_hbm, v_hbm, w_ref, o_ref, q_ref, k_ref, v_ref, sems):
    side = my_place()[1] ^ other
    copies = fetch(((q_hbm, q_ref), (k_hbm, k_ref), (v_hbm, v_ref)), side, sems, 2)
    rows = q_ref.shape[0]
    half = o_ref.shape[0]
    tile = 2 * STRETCH
    key = lax.broadcasted_iota(jnp.int32, (tile, tile), 0)
    tok = lax.broadcasted_iota(jnp.int32, (tile, tile), 1)
    low = jnp.logical_and(tok >= STRETCH, key < STRETCH)
    same = jnp.logical_and(key <= tok, jnp.logical_not(low))
    for n in range(half):
        if n % (half // 2) == 0:
            for copy in copies[3 * (2 * n // half) :][:3]:
                copy.wait()
        at = lanes(n)
        head = side * half + n
        value_t = v_ref[:, at].T
        levels = 1 + (rows // STRETCH).bit_length() - 1
        scales = [w_ref[level, pl.ds(head, 1), :] * level_factor(level) for level in range(levels)]
        for r in range(rows // tile):
            here = pl.ds(r * tile, tile)
            span = (r + 1) * tile
            scale = lambda level: scales[level][:, r * tile : (r + 1) * tile]
            score = lax.dot_general(
                k_ref[pl.ds(0, span), at], q_ref[here, at], (((1,), (1,)), ((), ())),
                preferred_element_type=F32,
            )
            parts = []
            for c in range(r):
                parts.append(score[c * tile : (c + 1) * tile] * scale(1 + (r ^ c).bit_length()))
            weight = jnp.where(same, scale(0), jnp.where(low, scale(1), 0.0))
            parts.append(score[r * tile :] * weight)
            weighted = jnp.concatenate([p.astype(BF16) for p in parts], axis=0)
            o_ref[n, :, here] = jnp.dot(value_t[:, :span], weighted, preferred_element_type=F32)


def local_part(other, queries, keys, values, weights):
    rows, width = queries.shape
    buffer = pltpu.VMEM((rows, width // 2), BF16)
    return kernel_call(
        functools.partial(local_kernel, other),
        jax.ShapeDtypeStruct((width // DK // 2, DK, rows), F32),
        [in_hbm(queries), in_hbm(keys), in_hbm(values), weights],
        flops=2 * rows * rows * width,
        spaces=[HBM, HBM, HBM, VMEM],
        scratch_shapes=[buffer, buffer, buffer, pltpu.SemaphoreType.DMA((6,))],
    )


def pair_kernel(keep_ref, first_ref, o_ref, rest_ref):
    partner = my_place()[2] ^ 1
    for i, d in enumerate((0, 2, 1, 3)):
        total = keep_ref[partner ^ d].astype(F32) + first_ref[partner ^ d].astype(F32)
        (o_ref if i < 2 else rest_ref)[i % 2] = total.astype(BF16)


def ahead_kernel(keep_ref, first_ref, one_ref, o_ref):
    n = my_place()[2] ^ 2
    o_ref[0] = (keep_ref[n].astype(F32) + first_ref[n].astype(F32) + one_ref[1].astype(F32)).astype(BF16)


def rest_kernel(keep_ref, first_ref, one_ref, other_ref, o_ref):
    n = my_place()[2]
    for i, (d, got) in enumerate(((3, other_ref[1]), (0, one_ref[0]), (1, other_ref[0]))):
        o_ref[i] = (keep_ref[n ^ d].astype(F32) + first_ref[n ^ d].astype(F32) + got.astype(F32)).astype(BF16)


def pick_kernel(keep_ref, first_ref, one_ref, two_ref, o_ref):
    n = my_place()[2]
    total = keep_ref[n].astype(F32) + first_ref[n].astype(F32) + one_ref[0].astype(F32) + two_ref[0].astype(F32)
    for g in range(o_ref.shape[0]):
        o_ref[g] = total.astype(BF16)


def sibling_sums(own, all_ref, o_ref, first):
    for b in range(all_ref.shape[0].bit_length() - 1):
        low = jnp.maximum(lax.shift_right_logical(own, b) - 1, 0) * 2**b
        total = all_ref[low].astype(F32)
        for i in range(1, 2**b):
            total = total + all_ref[low + i].astype(F32)
        o_ref[first + b] = total.astype(BF16)


def group_kernel(all_ref, late_ref, o_ref):
    sibling_sums(my_place()[3], all_ref, late_ref, 0)
    total = all_ref[0].astype(F32)
    for g in range(1, all_ref.shape[0]):
        total = total + all_ref[g].astype(F32)
    for r in range(o_ref.shape[0]):
        o_ref[r] = total.astype(BF16)


def run_kernel(all_ref, o_ref):
    sibling_sums(my_place()[0], all_ref, o_ref, 0)


def pack_kernel(keep_ref, first_ref, one_ref, other_ref, two_ref, rest_ref, *refs):
    o_ref = refs[-1]
    half = keep_ref.shape[0]
    n = my_place()[2]
    o_ref[pl.ds(0, half)] = jnp.where(my_place()[1] == 1, first_ref[...], keep_ref[...])
    for i in range(2):
        o_ref[half + (n ^ 2 * i)] = one_ref[i]
        o_ref[half + (n ^ 1 ^ 2 * i)] = other_ref[i]
    o_ref[2 * half + n] = two_ref[0]
    for d in range(1, half):
        o_ref[2 * half + (n ^ d)] = rest_ref[d - 1]
    start = 3 * half
    for ref in refs[:-1]:
        o_ref[pl.ds(start, ref.shape[0])] = ref[...]
        start += ref.shape[0]


def slot_head(slot):
    return my_place()[2] ^ (slot // 2 | slot % 2 * 2)


def add_levels(q_ref, w_ref, total, head, found, bits, local_bits):
    part = lax.dot_general(found, q_ref[:, lanes(head)], (((1,), (1,)), ((), ())), preferred_element_type=F32)
    for i, bit in enumerate(bits):
        level = 1 + local_bits + bit
        live = (lax.shift_right_logical(my_place()[4], bit) & 1) == 1
        gain = jnp.where(live, level_factor(level), 0.0)
        total = total + part[i * DK : (i + 1) * DK] * (w_ref[level, pl.ds(head, 1), :] * gain)
    return total


def near_kernel(other, mid, late, local_bits, q_ref, a_ref, w_ref, found_ref, t_ref, done_ref):
    half = a_ref.shape[0]
    for slot in range(half):
        n = slot_head(slot)
        head = (my_place()[1] ^ other) * half + n
        found = [found_ref[level * half + n] for level in range(3)]
        found.append(found_ref[pl.ds(3 * half + slot * mid, mid)].reshape(mid * DK, DK))
        bits = 3 + mid
        if slot < 2:
            found.append(found_ref[pl.ds((3 + mid) * half + slot * late, late)].reshape(late * DK, DK))
            bits += late
        found = jnp.concatenate(found, axis=0)
        total = add_levels(q_ref, w_ref, a_ref[n], head, found, range(bits), local_bits)
        if slot < 2:
            done_ref[slot] = total.astype(BF16).T
        else:
            t_ref[slot - 2] = total


def add_far(other, mid, late, local_bits, q_ref, t_ref, w_ref, found_ref, out_hbm, o_ref, sems, copies):
    count = t_ref.shape[0]
    for i in range(count):
        head = (my_place()[1] ^ other) * 2 * count + slot_head(2 + i)
        found = found_ref[pl.ds(i * late, late)].reshape(late * DK, DK)
        bits = range(3 + mid, 3 + mid + late)
        total = add_levels(q_ref, w_ref, t_ref[i], head, found, bits, local_bits)
        o_ref[i] = total.astype(BF16).T
        copies.append(pltpu.make_async_copy(o_ref.at[i], out_hbm.at[:, lanes(head)], sems.at[len(copies)]))
        copies[-1].start()
    for copy in copies:
        copy.wait()


def far_mine_kernel(mid, late, local_bits, q_ref, t_ref, w_ref, found_ref, own_ref, their_ref, out_hbm, o_ref, sems):
    copies = []
    for other, ref in enumerate((own_ref, their_ref)):
        for slot in range(2):
            head = (my_place()[1] ^ other) * 2 * t_ref.shape[0] + slot_head(slot)
            copies.append(pltpu.make_async_copy(ref.at[slot], out_hbm.at[:, lanes(head)], sems.at[len(copies)]))
            copies[-1].start()
    add_far(0, mid, late, local_bits, q_ref, t_ref, w_ref, found_ref, out_hbm, o_ref, sems, copies)


def far_theirs_kernel(mid, late, local_bits, q_ref, t_ref, w_ref, found_ref, before_hbm, out_hbm, o_ref, sems):
    add_far(1, mid, late, local_bits, q_ref, t_ref, w_ref, found_ref, out_hbm, o_ref, sems, [])


def attend(queries, keys, values, level_weights):
    rows, width = queries.shape
    heads = width // DK
    half = heads // 2
    local_bits = (rows // STRETCH).bit_length() - 1
    blocks = lax.axis_size("ctx")
    runs = lax.axis_size("grp")
    groups = blocks // 8
    send, own_keys, own_values = send_states(keys, values)
    first = swap(send, "ctx", 1)
    keep = kernel_call(put_states, states(half), [own_keys, own_values], flops=rows * DK * width)
    pair, pair_rest = kernel_call(pair_kernel, [states(2), states(half - 2)], [keep, first])
    one_z = swap(pair, "ctx", 2)
    one_rest = swap(pair_rest, "ctx", 2)
    ahead = kernel_call(ahead_kernel, states(1), [keep, first, one_z])
    two_z = swap(ahead, "ctx", 4)
    rest = kernel_call(rest_kernel, states(half - 1), [keep, first, one_z, one_rest])
    two_rest = swap(rest, "ctx", 4)
    locals_ = [local_part(other, queries, keys, values, level_weights) for other in (0, 1)]
    picked = kernel_call(pick_kernel, states(groups), [keep, first, one_z, two_z])
    members = [[low + 8 * g for g in range(groups)] for low in range(8)]
    group_sums = lax.all_to_all(picked, "ctx", 0, 0, axis_index_groups=members, tiled=True)
    mid = groups.bit_length() - 1
    mid0, spread = kernel_call(group_kernel, [states(mid), states(runs)], [group_sums])
    run_states = lax.all_to_all(spread, "grp", 0, 0, tiled=True)

    mid1 = swap(mid0, "ctx", 4)
    mid23 = swap(jnp.concatenate([mid0, mid1], axis=0), "ctx", 2)
    late = runs.bit_length() - 1
    slot0 = kernel_call(run_kernel, states(late), [run_states])

    slot1 = swap(slot0, "ctx", 4)
    slot23 = swap(jnp.concatenate([slot0, slot1], axis=0), "ctx", 2)
    mine = kernel_call(
        pack_kernel,
        states((3 + mid) * half + 2 * late),
        [keep, first, one_z, one_rest, two_z, two_rest, mid0, mid1, mid23, slot0, slot1],
    )
    theirs = swap(mine, "ctx", 1)
    out_type = jax.ShapeDtypeStruct((rows, width), BF16)

    def near(other, found):
        return kernel_call(
            functools.partial(near_kernel, other, mid, late, local_bits),
            [jax.ShapeDtypeStruct((2, DK, rows), F32), jax.ShapeDtypeStruct((2, rows, DK), BF16)],
            [queries, locals_[other], level_weights, found],
            limit=24,
            flops=2 * rows * DK * DK * (half * (3 + mid) + 2 * late),
        )

    def far(kernel, operands, spaces, copies, **more):
        return kernel_call(
            functools.partial(kernel, mid, late, local_bits),
            out_type,
            operands,
            flops=4 * rows * DK * DK * late,
            spaces=spaces,
            out_specs=HBM,
            scratch_shapes=[pltpu.VMEM((2, rows, DK), BF16), pltpu.SemaphoreType.DMA((copies,))],
            **more,
        )

    own_total, own_done = near(0, mine)
    other_total, other_done = near(1, theirs)
    their23 = swap(slot23, "ctx", 1)
    out = far(far_mine_kernel, [queries, own_total, level_weights, slot23, own_done, other_done], [VMEM] * 6, 6)
    return far(
        far_theirs_kernel, [queries, other_total, level_weights, their23, out],
        [VMEM] * 4 + [HBM], 2, input_output_aliases={4: 0},
    )


def solution(mesh):
    return jax.shard_map(
        attend,
        mesh=mesh,
        in_specs=(
            P(("grp", "ctx"), None),
            P(("grp", "ctx"), None),
            P(("grp", "ctx"), None),
            P(None, None, ("grp", "ctx")),
        ),
        out_specs=P(("grp", "ctx"), None),
        check_vma=False,
    )
```
